32 devices in a mesh: row: 4 (over y, x), col: 8 (over z, core).
Axes of the slice: x: 2, y: 2, z: 4, core: 2. Of those that a mesh axis runs over, the one named last changes fastest.
Arguments:
- tiles: float32 [4, 8, 3, 128, 64, 128], P('row', 'col'), may hold values from -0.0625 to 0.0625
- tile_coords: int32 [4, 8, 3, 2, 256], P('row', 'col'), may hold values from 0 to 15, as said below
- tile_count: int32 [4, 8, 3], P('row', 'col'), may hold values from 32 to 256, as said below
- seeds: int32 [128], replicated, may hold values from 0 to 4095
- chain: int32 [3], replicated, may hold values from 0 to 2
Outputs:
- answers: float32 [4096, 128], P(('row', 'col'))
The draws below stay inside these ranges and needn't reach their ends.
Inputs may be any that keep to these rules, and one draw needn't show every extreme that they name: tile_coords[..., 0, :] is below 8 * 2 and tile_coords[..., 1, :] below 4 * 2; pairs may repeat. `tile_count`: each count is 256 divided by 1, 2, 4 or 8; for every relation some device has all 256 slots live.
All inputs are finite; a program needn't handle non-finite values.
Results may differ from the reference program's by a relative error of at most 0.0003.
Values sent between devices are 32-bit elements; how exact they have to be, the bound alone decides.
No kernel may reach another device: no remote copies, remote signals or barrier semaphores. Data moves between devices by JAX's collectives and lax.ppermute only.
A program may use at most 128 MiB of HBM per device.

```python
import jax
import jax.numpy as jnp
from jax import lax

QUERIES = 128
TILE = 64
BLOCKS_DEV = 2
TILES_DEV = 256
RELATIONS = 3
HOPS = 3
ENTITIES = 4096
N_ROW = 4
N_COL = 8


def draw_tile_coords(key, part):
    key_rows, key_left, key_right, key_order = jax.random.split(key, 4)
    shape = (N_ROW, N_COL, RELATIONS, TILES_DEV)
    span_rows = N_COL * BLOCKS_DEV
    span_cols = N_ROW * BLOCKS_DEV
    row_index = jax.random.randint(key_rows, shape, 0, span_rows, dtype=jnp.int32)
    left = jax.random.randint(key_left, shape, 0, span_cols, dtype=jnp.int32)
    right = jax.random.randint(key_right, shape, 0, span_cols, dtype=jnp.int32)
    order = jax.random.permutation(key_order, span_cols).astype(jnp.int32)
    col_index = order[left * right // span_cols]
    row_index = row_index.at[..., 0].set(span_rows - 1)
    col_index = col_index.at[..., 1].set(span_cols - 1)
    return jnp.stack([row_index, col_index], axis=3).astype(jnp.int32)


def draw_tile_count(key, part):
    key_shift, key_full = jax.random.split(key, 2)
    shift = jax.random.randint(key_shift, (N_ROW * N_COL, RELATIONS), 0, 4, dtype=jnp.int32)
    counts = jnp.floor_divide(TILES_DEV, jnp.left_shift(jnp.ones_like(shift), shift))
    fullest = jax.random.randint(key_full, (RELATIONS,), 0, N_ROW * N_COL, dtype=jnp.int32)
    counts = counts.at[fullest, jnp.arange(RELATIONS)].set(TILES_DEV)
    return counts.reshape(N_ROW, N_COL, RELATIONS).astype(jnp.int32)


def plant(values, own_key, low, top_value):
    spot = [jax.random.randint(jax.random.fold_in(own_key, axis), (), 0, length) for axis, length in enumerate(values.shape)]
    main_axis = values.shape.index(max(values.shape))
    beside = spot[:main_axis] + [(spot[main_axis] + 1) % values.shape[main_axis]] + spot[main_axis + 1:]
    return values.at[tuple(spot)].set(low).at[tuple(beside)].set(top_value)


def steps_of(rng, dims, cuts, least, largest):
    factor_of, own = 1.0, jax.random.fold_in(rng, 6)
    for axis_at, parts in cuts:
        draws = jnp.exp(jax.random.uniform(jax.random.fold_in(own, axis_at), (parts,), jnp.float32, least / len(cuts), largest / len(cuts)))
        factor_of = factor_of * jnp.repeat(draws, dims[axis_at] // parts).reshape([-1 if axis == axis_at else 1 for axis in range(len(dims))])
    return factor_of


def centred(key, extent, scale, reach, pieces=(), kind=jnp.bfloat16):
    loudness = steps_of(key, extent, pieces, -0.22, 0.18) if pieces else 1.0
    drawn = jax.random.normal(key, extent, jnp.float32) * scale * loudness
    return jnp.minimum(jnp.maximum(drawn, -reach), reach).astype(kind)


def setup_inputs(seed: int = 0) -> dict:
    arg_keys = jax.random.split(jax.random.key(seed), 6)
    return {
        "tiles": centred(arg_keys[0], (N_ROW, N_COL, RELATIONS, TILES_DEV // 2, TILE, 2 * TILE), (TILE * TILES_DEV // BLOCKS_DEV) ** -0.5, 0.0625, ((0, 4), (1, 8)), jnp.float32),
        "tile_coords": draw_tile_coords(jax.random.fold_in(arg_keys[5], 71), 0),
        "tile_count": draw_tile_count(jax.random.fold_in(arg_keys[5], 71), 0),
        "seeds": plant(jax.random.randint(arg_keys[3], (QUERIES,), 0, ENTITIES), jax.random.fold_in(arg_keys[3], 1), 0, ENTITIES - 1).astype(jnp.int32),
        "chain": jax.random.randint(arg_keys[4], (HOPS,), 0, RELATIONS).astype(jnp.int32),
    }


def paired_products(pair_values, picked):
    pair_total = pair_values.shape[0]
    split_values = pair_values.reshape(pair_total, TILE, 2, TILE)
    split_states = picked.reshape(pair_total, 2, TILE, QUERIES)
    product = jnp.einsum('sahb,shbq->shaq', split_values, split_states, precision=lax.Precision.HIGHEST)
    return product.reshape(pair_total * 2, TILE, QUERIES)

def apply_relation(state, tiles, tile_coords, tile_count, relation):
    column_view = state.reshape(N_ROW, N_COL, BLOCKS_DEV * TILE, QUERIES)
    out_blocks = N_COL * BLOCKS_DEV
    zero_index = jnp.zeros((), jnp.int32)
    relation = relation.astype(jnp.int32)

    def one_row(grid_row):
        grid_row = grid_row.astype(jnp.int32)

        def one_col(total, grid_col):
            grid_col = grid_col.astype(jnp.int32)
            segment = lax.dynamic_index_in_dim(column_view, grid_col, 1, keepdims=False)
            blocks = segment.reshape(N_ROW * BLOCKS_DEV, TILE, QUERIES)
            values = lax.dynamic_slice(tiles, (grid_row, grid_col, relation, zero_index, zero_index, zero_index), (1, 1, 1, TILES_DEV // 2, TILE, 2 * TILE))[0, 0, 0]
            coords = lax.dynamic_slice(tile_coords, (grid_row, grid_col, relation, zero_index, zero_index), (1, 1, 1, 2, TILES_DEV))[0, 0, 0]
            live_count = lax.dynamic_slice(tile_count, (grid_row, grid_col, relation), (1, 1, 1))[0, 0, 0]
            picked = blocks[coords[1]]
            product = paired_products(values, picked)
            live = jnp.arange(TILES_DEV, dtype=jnp.int32) < live_count
            product = jnp.where(live[:, None, None], product, jnp.zeros_like(product))
            return (total + jax.ops.segment_sum(product, coords[0], num_segments=out_blocks), None)
        start = jnp.zeros((out_blocks, TILE, QUERIES), state.dtype)
        total, _ = lax.scan(one_col, start, jnp.arange(N_COL, dtype=jnp.int32))
        return total
    rows_out = lax.map(one_row, jnp.arange(N_ROW, dtype=jnp.int32))
    return rows_out.reshape(N_ROW * N_COL * BLOCKS_DEV * TILE, QUERIES)

def reference(tiles, tile_coords, tile_count, seeds, chain):
    entity_ids = jnp.arange(ENTITIES, dtype=jnp.int32)
    state = (entity_ids[:, None] == seeds.astype(jnp.int32)[None, :]).astype(tiles.dtype)
    for step_index in range(HOPS):
        state = apply_relation(state, tiles, tile_coords, tile_count, chain[step_index].astype(jnp.int32))
    totals = lax.optimization_barrier(jnp.sum(state * state, axis=0))
    return state * lax.rsqrt(totals / ENTITIES + 1e-06)
```

```python
import functools

import jax
import jax.numpy as jnp
from jax import lax
from jax.experimental import pallas as pl
from jax.experimental.pallas import tpu as pltpu
from jax.sharding import PartitionSpec as P

QUERIES = 128
TILE = 64
BLOCKS_DEV = 2
HOPS = 3
ROWS_DEV = BLOCKS_DEV * TILE
LANES = 128
MIN_SHARE = 8


def place_tiles(step, in_pairs, flips, chain, counts, coords, tiles, buf, coord_buf, sems, coord_sem, accs):
    pairs = tiles.shape[1]
    chunk = pairs // MIN_SHARE
    relation = chain[step]
    live_chunks = counts[0, 0, relation] // (2 * chunk)
    row_flip, col_flip = flips[0], flips[1]
    copy_coords = pltpu.make_async_copy(coords.at[relation], coord_buf, coord_sem)
    copy_coords.start()

    def chunk_copy(index):
        span = pl.ds(index * chunk, chunk)
        return pltpu.make_async_copy(tiles.at[relation, span], buf.at[span], sems.at[index])

    for index in range(MIN_SHARE):
        @pl.when(index < live_chunks)
        def _(index=index):
            chunk_copy(index).start()

    acc_even, acc_odd = accs[0], accs[-1]
    blocks = acc_even.shape[0]

    @pl.loop(0, blocks // 4)
    def _(b):
        for u in range(4):
            for acc in accs:
                acc[b * 4 + u] = jnp.zeros((TILE, LANES), jnp.float32)

    half_of_lane = lax.broadcasted_iota(jnp.int32, (TILE, LANES), 1) // TILE
    copy_coords.wait()

    def add_pair(t):
        values = buf[t]
        rolled = pltpu.roll(values, TILE, 1)
        for odd, acc in ((0, acc_even), (1, acc_odd)):
            i = coord_buf[0, 2 * t + odd] ^ row_flip
            j = coord_buf[1, 2 * t + odd] ^ col_flip
            half = j & 1
            at = i * in_pairs + (j >> 1)
            moved = jnp.where(half == odd, values, rolled)
            acc[at] = acc[at] + jnp.where(half_of_lane == half, moved, 0.0)

    @pl.loop(0, live_chunks)
    def _(index):
        chunk_copy(index).wait()

        @pl.loop(0, chunk // 4)
        def _(t):
            for u in range(4):
                add_pair(index * chunk + t * 4 + u)


def split(x):
    high = x.astype(jnp.bfloat16)
    return high, (x - high.astype(jnp.float32)).astype(jnp.bfloat16)


def fold(accs, out_blocks, in_pairs, highs, lows):
    @pl.loop(0, out_blocks)
    def _(i):
        away = (i // BLOCKS_DEV) & 1
        at = pl.multiple_of((i // (2 * BLOCKS_DEV)) * ROWS_DEV + (i & 1) * TILE, TILE)
        for jp in range(in_pairs):
            value = accs[0][i * in_pairs + jp]
            if len(accs) == 2:
                value = value + accs[1][i * in_pairs + jp]
            high, low = split(value)
            highs[away, pl.ds(at, TILE), jp * LANES:(jp + 1) * LANES] = high
            lows[away, pl.ds(at, TILE), jp * LANES:(jp + 1) * LANES] = low


def first_kernel(out_blocks, in_pairs, chain, counts, flips, targets, coords, tiles, keep, send,
                 buf, coord_buf, sems, coord_sem, highs, lows, *accs):
    place_tiles(0, in_pairs, flips, chain, counts, coords, tiles, buf, coord_buf, sems, coord_sem, accs)
    fold(accs, out_blocks, in_pairs, highs, lows)
    depth = in_pairs * LANES
    entity = lax.broadcasted_iota(jnp.int32, (depth, QUERIES), 0)
    states = (entity == targets[...]).astype(jnp.float32).astype(jnp.bfloat16)
    for away, out in ((1, send), (0, keep)):
        out[...] = jnp.dot(highs[away], states, preferred_element_type=jnp.float32) + jnp.dot(
            lows[away], states, preferred_element_type=jnp.float32)


def dense_kernel(step, out_blocks, in_pairs, chain, counts, flips, coords, tiles, highs, lows,
                 buf, coord_buf, sems, coord_sem, *accs):
    place_tiles(step, in_pairs, flips, chain, counts, coords, tiles, buf, coord_buf, sems, coord_sem, accs)
    fold(accs, out_blocks, in_pairs, highs, lows)


def product_kernel(parts, highs, lows, *refs):
    pieces, (keep, send, weights) = refs[:parts], refs[parts:]
    for k, piece in enumerate(pieces):
        high, low = split(piece[...])
        weights[k * ROWS_DEV:(k + 1) * ROWS_DEV, :QUERIES] = high
        weights[k * ROWS_DEV:(k + 1) * ROWS_DEV, QUERIES:] = low
    for away, out in ((1, send), (0, keep)):
        both = jnp.dot(highs[away], weights[...], preferred_element_type=jnp.float32)
        rest = jnp.dot(lows[away], weights[:, :QUERIES], preferred_element_type=jnp.float32)
        out[...] = both[:, :QUERIES] + (both[:, QUERIES:] + rest)


def shards(tiles, tile_coords, tile_count, seeds, chain):
    row_total = lax.axis_size("row")
    col_total = lax.axis_size("col")
    my_row = lax.axis_index("row")
    my_col = lax.axis_index("col")
    out_blocks = col_total * BLOCKS_DEV
    in_pairs = row_total
    depth_total = col_total // 2
    rows_out = depth_total * ROWS_DEV
    rows_in = in_pairs * LANES
    relations, pairs = tiles.shape[2], tiles.shape[3]
    f32, bf16 = jnp.float32, jnp.bfloat16

    tiles = tiles.reshape(relations, pairs, TILE, 2 * TILE)
    coords = tile_coords.reshape(relations, 2, 2 * pairs)
    flips = jnp.stack([my_col * BLOCKS_DEV, my_row * BLOCKS_DEV]).astype(jnp.int32)
    block = seeds // ROWS_DEV
    targets = jnp.where(block % col_total == my_col,
                        ((block // col_total) ^ my_row) * ROWS_DEV + seeds % ROWS_DEV, -1)[None, :]

    small = out_blocks * in_pairs * TILE * LANES * 4 <= 4 << 20
    smem = pl.BlockSpec(memory_space=pltpu.SMEM)
    vmem = pl.BlockSpec(memory_space=pltpu.VMEM)
    hbm = pl.BlockSpec(memory_space=pl.ANY)
    params = pltpu.CompilerParams(vmem_limit_bytes=60 << 20)
    work = [
        pltpu.VMEM((pairs, TILE, 2 * TILE), f32),
        pltpu.SMEM((2, 2 * pairs), jnp.int32),
        pltpu.SemaphoreType.DMA((MIN_SHARE,)),
        pltpu.SemaphoreType.DMA(()),
    ]
    accs = [pltpu.VMEM((out_blocks * in_pairs, TILE, LANES), f32)] * (2 if small else 1)
    dense = jax.ShapeDtypeStruct((2, rows_out, rows_in), bf16)
    partial = jax.ShapeDtypeStruct((rows_out, QUERIES), f32)

    def first():
        return pl.pallas_call(
            functools.partial(first_kernel, out_blocks, in_pairs),
            out_shape=[partial, partial],
            in_specs=[smem, smem, smem, vmem, hbm, hbm],
            out_specs=[vmem, vmem],
            scratch_shapes=work + [pltpu.VMEM(dense.shape, bf16)] * 2 + accs,
            compiler_params=params,
            name="first",
        )(chain, tile_count, flips, targets, coords, tiles)

    def densify(step):
        return pl.pallas_call(
            functools.partial(dense_kernel, step, out_blocks, in_pairs),
            out_shape=[dense, dense],
            in_specs=[smem, smem, smem, hbm, hbm],
            out_specs=[vmem, vmem],
            scratch_shapes=work + accs,
            compiler_params=params,
            cost_estimate=pl.CostEstimate(flops=0, bytes_accessed=8 << 20, transcendentals=0),
            name=f"densify{step}",
        )(chain, tile_count, flips, coords, tiles)

    def product(highs, lows, pieces):
        return pl.pallas_call(
            functools.partial(product_kernel, len(pieces)),
            out_shape=[partial, partial],
            in_specs=[vmem] * (2 + len(pieces)),
            out_specs=[vmem, vmem],
            scratch_shapes=[pltpu.VMEM((rows_in, 2 * QUERIES), bf16)],
            compiler_params=params,
            name="product",
        )(highs, lows, *pieces)

    def swap(x, axis, size, flip):
        return lax.ppermute(x, axis, [(i, i ^ flip) for i in range(size)])

    keep, send = first()
    for step in range(HOPS):
        summed = keep + swap(send, "col", col_total, 1)
        arrived = [
            swap(summed[k * ROWS_DEV:(k + 1) * ROWS_DEV], "col", col_total, 2 * k)
            for k in range(1, depth_total)
        ]
        owned = summed[:ROWS_DEV]
        for part in arrived:
            owned = owned + part
        if step + 1 < HOPS:
            highs, lows = densify(step + 1)
            pieces = [owned] + [swap(owned, "row", row_total, k) for k in range(1, row_total)]
            keep, send = product(highs, lows, pieces)

    squares = jnp.sum(owned * owned, axis=0, keepdims=True)
    devices = row_total * col_total
    shared = lax.all_to_all(
        jnp.broadcast_to(squares, (devices, QUERIES)), ("row", "col"), 0, 0, tiled=True)
    totals = jnp.sum(shared, axis=0)
    return owned * lax.rsqrt(totals / (devices * ROWS_DEV) + 1e-06)


def solution(mesh):
    in_specs = (
        P("row", "col", None, None, None, None),
        P("row", "col", None, None, None),
        P("row", "col", None),
        P(),
        P(),
    )
    out_specs = P(("row", "col"), None)
    return jax.shard_map(shards, mesh=mesh, in_specs=in_specs, out_specs=out_specs, check_vma=False)
```

```python
import functools

import jax
import jax.numpy as jnp
from jax import lax
from jax.experimental import pallas as pl
from jax.experimental.pallas import tpu as pltpu
from jax.sharding import PartitionSpec as P


QUERIES = 128
TILE = 64
BLOCKS_DEV = 2
HOPS = 3
ROWS_DEV = BLOCKS_DEV * TILE
LANES = 128
MIN_SHARE = 8


def place_tiles(step, in_pairs, chain, counts, coords, tiles, buf, coord_buf, sems, coord_sem, accs):
    pairs = tiles.shape[1]
    chunk = pairs // MIN_SHARE
    relation = chain[step]
    live_chunks = counts[0, 0, relation] // (2 * chunk)
    row_flip = lax.axis_index("col") * BLOCKS_DEV
    col_flip = lax.axis_index("row") * BLOCKS_DEV
    copy_coords = pltpu.make_async_copy(coords.at[relation], coord_buf, coord_sem)
    copy_coords.start()

    def chunk_copy(index):
        span = pl.ds(index * chunk, chunk)
        return pltpu.make_async_copy(tiles.at[relation, span], buf.at[span], sems.at[index])

    for index in range(MIN_SHARE):
        @pl.when(index < live_chunks)
        def _(index=index):
            chunk_copy(index).start()

    acc_even, acc_odd = accs[0], accs[-1]
    blocks = acc_even.shape[0]

    @pl.loop(0, blocks // 4)
    def _(b):
        for u in range(4):
            for acc in accs:
                acc[b * 4 + u] = jnp.zeros((TILE, LANES), jnp.float32)

    half_of_lane = lax.broadcasted_iota(jnp.int32, (TILE, LANES), 1) // TILE
    copy_coords.wait()

    def add_pair(t):
        values = buf[t]
        rolled = pltpu.roll(values, TILE, 1)
        for odd, acc in ((0, acc_even), (1, acc_odd)):
            i = coord_buf[0, 2 * t + odd] ^ row_flip
            j = coord_buf[1, 2 * t + odd] ^ col_flip
            half = j & 1
            at = i * in_pairs + (j >> 1)
            moved = jnp.where(half == odd, values, rolled)
            acc[at] = acc[at] + jnp.where(half_of_lane == half, moved, 0.0)

    @pl.loop(0, live_chunks)
    def _(index):
        chunk_copy(index).wait()

        @pl.loop(0, chunk // 4)
        def _(t):
            for u in range(4):
                add_pair(index * chunk + t * 4 + u)


def split(x):
    high = x.astype(jnp.bfloat16)
    return high, (x - high.astype(jnp.float32)).astype(jnp.bfloat16)


def fold(accs, out_blocks, in_pairs, highs, lows):
    @pl.loop(0, out_blocks)
    def _(i):
        away = (i // BLOCKS_DEV) & 1
        at = pl.multiple_of((i // (2 * BLOCKS_DEV)) * ROWS_DEV + (i & 1) * TILE, TILE)
        for jp in range(in_pairs):
            value = accs[0][i * in_pairs + jp]
            if len(accs) == 2:
                value = value + accs[1][i * in_pairs + jp]
            high, low = split(value)
            highs[away, pl.ds(at, TILE), jp * LANES:(jp + 1) * LANES] = high
            lows[away, pl.ds(at, TILE), jp * LANES:(jp + 1) * LANES] = low


def first_kernel(out_blocks, in_pairs, chain, counts, seeds, coords, tiles, keep, send,
                 buf, coord_buf, sems, coord_sem, highs, lows, *accs):
    place_tiles(0, in_pairs, chain, counts, coords, tiles, buf, coord_buf, sems, coord_sem, accs)
    fold(accs, out_blocks, in_pairs, highs, lows)
    depth = in_pairs * LANES
    cols = out_blocks // BLOCKS_DEV
    block = seeds[...] // ROWS_DEV
    target = ((block // cols) ^ lax.axis_index("row")) * ROWS_DEV + seeds[...] % ROWS_DEV
    target = jnp.where(block % cols == lax.axis_index("col"), target, -1)
    entity = lax.broadcasted_iota(jnp.int32, (depth, QUERIES), 0)
    states = (entity == target).astype(jnp.float32).astype(jnp.bfloat16)
    for away, out in ((1, send), (0, keep)):
        out[...] = jnp.dot(highs[away], states, preferred_element_type=jnp.float32) + jnp.dot(
            lows[away], states, preferred_element_type=jnp.float32)


def dense_kernel(step, out_blocks, in_pairs, chain, counts, coords, tiles, highs, lows,
                 buf, coord_buf, sems, coord_sem, *accs):
    place_tiles(step, in_pairs, chain, counts, coords, tiles, buf, coord_buf, sems, coord_sem, accs)
    fold(accs, out_blocks, in_pairs, highs, lows)


def product_kernel(parts, highs, lows, *refs):
    pieces, (keep, send, weights) = refs[:parts], refs[parts:]
    for k, piece in enumerate(pieces):
        high, low = split(piece[...])
        weights[k * ROWS_DEV:(k + 1) * ROWS_DEV, :QUERIES] = high
        weights[k * ROWS_DEV:(k + 1) * ROWS_DEV, QUERIES:] = low
    for away, out in ((1, send), (0, keep)):
        both = jnp.dot(highs[away], weights[...], preferred_element_type=jnp.float32)
        rest = jnp.dot(lows[away], weights[:, :QUERIES], preferred_element_type=jnp.float32)
        out[...] = both[:, :QUERIES] + (both[:, QUERIES:] + rest)


def shards(tiles, tile_coords, tile_count, seeds, chain):
    row_total = lax.axis_size("row")
    col_total = lax.axis_size("col")
    out_blocks = col_total * BLOCKS_DEV
    in_pairs = row_total
    depth_total = col_total // 2
    rows_out = depth_total * ROWS_DEV
    rows_in = in_pairs * LANES
    relations, pairs = tiles.shape[2], tiles.shape[3]
    f32, bf16 = jnp.float32, jnp.bfloat16

    tiles = tiles.reshape(relations, pairs, TILE, 2 * TILE)
    coords = tile_coords.reshape(relations, 2, 2 * pairs)
    seeds = seeds[None, :]

    small = out_blocks * in_pairs * TILE * LANES * 4 <= 4 << 20
    smem = pl.BlockSpec(memory_space=pltpu.SMEM)
    vmem = pl.BlockSpec(memory_space=pltpu.VMEM)
    hbm = pl.BlockSpec(memory_space=pltpu.HBM)
    dense_bytes = out_blocks * in_pairs * TILE * LANES * 4
    params = pltpu.CompilerParams(
        vmem_limit_bytes=(3 if small else 2) * dense_bytes + pairs * TILE * LANES * 4 + (6 << 20))
    product_params = pltpu.CompilerParams(vmem_limit_bytes=dense_bytes + (8 << 20))
    work = [
        pltpu.VMEM((pairs, TILE, 2 * TILE), f32),
        pltpu.SMEM((2, 2 * pairs), jnp.int32),
        pltpu.SemaphoreType.DMA((MIN_SHARE,)),
        pltpu.SemaphoreType.DMA(()),
    ]
    accs = [pltpu.VMEM((out_blocks * in_pairs, TILE, LANES), f32)] * (2 if small else 1)
    dense = pltpu.VMEM((2, rows_out, rows_in), bf16)
    partial = pltpu.VMEM((rows_out, QUERIES), f32)

    def local(x):
        return pltpu.with_memory_space_constraint(x, pltpu.VMEM)

    def remain(x):
        return pltpu.with_memory_space_constraint(x, pltpu.HBM)

    given = [remain(x) for x in (chain, tile_count, seeds, coords, tiles)]

    def first():
        return pl.pallas_call(
            functools.partial(first_kernel, out_blocks, in_pairs),
            out_shape=[partial, partial],
            in_specs=[smem, smem, vmem, hbm, hbm],
            out_specs=[vmem, vmem],
            scratch_shapes=work + [pltpu.VMEM(dense.shape, bf16)] * 2 + accs,
            compiler_params=params,
            name="first",
        )(*given)

    def densify(step):
        return pl.pallas_call(
            functools.partial(dense_kernel, step, out_blocks, in_pairs),
            out_shape=[dense, dense],
            in_specs=[smem, smem, hbm, hbm],
            out_specs=[vmem, vmem],
            scratch_shapes=work + accs,
            compiler_params=params,
            cost_estimate=pl.CostEstimate(flops=0, bytes_accessed=8 << 20, transcendentals=0),
        )(*given[:2], *given[3:])

    def product(highs, lows, pieces):
        return pl.pallas_call(
            functools.partial(product_kernel, len(pieces)),
            out_shape=[partial, partial],
            in_specs=[vmem] * (2 + len(pieces)),
            out_specs=[vmem, vmem],
            scratch_shapes=[pltpu.VMEM((rows_in, 2 * QUERIES), bf16)],
            compiler_params=product_params,
            name="product",
        )(local(highs), local(lows), *map(local, pieces))

    def swap(x, axis, size, flip):
        return lax.ppermute(x, axis, [(i, i ^ flip) for i in range(size)])

    keep, send = first()
    for step in range(HOPS):
        summed = keep + swap(send, "col", col_total, 1)
        arrived = [
            swap(summed[k * ROWS_DEV:(k + 1) * ROWS_DEV], "col", col_total, 2 * k)
            for k in range(1, depth_total)
        ]
        if step + 1 < HOPS:
            highs, lows = densify(step + 1)
        owned = summed[:ROWS_DEV]
        for part in arrived:
            owned = owned + part
        if step + 1 < HOPS:
            pieces = [owned] + [swap(owned, "row", row_total, k) for k in range(1, row_total)]
            keep, send = product(highs, lows, pieces)

    squares = jnp.sum(owned * owned, axis=0, keepdims=True)
    devices = row_total * col_total
    shared = lax.all_to_all(
        jnp.broadcast_to(squares, (devices, QUERIES)), ("row", "col"), 0, 0, tiled=True)
    totals = jnp.sum(shared, axis=0)
    return owned * lax.rsqrt(totals / (devices * ROWS_DEV) + 1e-06)


def solution(mesh):
    in_specs = (
        P("row", "col", None, None, None, None),
        P("row", "col", None, None, None),
        P("row", "col", None),
        P(),
        P(),
    )
    out_specs = P(("row", "col"), None)
    return jax.shard_map(shards, mesh=mesh, in_specs=in_specs, out_specs=out_specs, check_vma=False)
```

```python
import functools

import jax
import jax.numpy as jnp
from jax import lax
from jax.experimental import pallas as pl
from jax.experimental.pallas import tpu as pltpu
from jax.sharding import PartitionSpec as P


QUERIES = 128
TILE = 64
BLOCKS_DEV = 2
HOPS = 3
ROWS_DEV = BLOCKS_DEV * TILE
LANES = 128
MIN_SHARE = 8


def place_tiles(step, in_pairs, chain, counts, coords, tiles, buf, coord_buf, spots, sems, acc):
    pairs = tiles.shape[1]
    chunk = pairs // MIN_SHARE
    blocks = acc.shape[0] // 2
    relation = chain[step]
    live_chunks = counts[0, 0, relation] // (2 * chunk)
    copy_coords = pltpu.make_async_copy(coords.at[relation], coord_buf, sems.at[MIN_SHARE])
    copy_coords.start()

    def chunk_copy(index):
        span = pl.ds(index * chunk, chunk)
        return pltpu.make_async_copy(tiles.at[relation, span], buf.at[span], sems.at[index])

    for index in range(MIN_SHARE):
        @pl.when(index < live_chunks)
        def _(index=index):
            chunk_copy(index).start()

    copy_coords.wait()
    slot = lax.broadcasted_iota(jnp.int32, (1, 2 * pairs), 1)
    i = coord_buf[0:1, :] ^ (lax.axis_index("col") * BLOCKS_DEV)
    j = coord_buf[1:2, :] ^ (lax.axis_index("row") * BLOCKS_DEV)
    coord_buf[0:1, :] = ((j ^ slot) & 1) * blocks + i * in_pairs + (j >> 1)
    copy_spots = pltpu.make_async_copy(coord_buf.at[pl.ds(0, 1)], spots, sems.at[MIN_SHARE])
    copy_spots.start()

    @pl.loop(0, 2 * blocks // 8)
    def _(b):
        for u in range(8):
            acc[b * 8 + u] = jnp.zeros((TILE, LANES), jnp.float32)

    left = lax.broadcasted_iota(jnp.int32, (TILE, LANES), 1) < TILE
    copy_spots.wait()

    def add_pair(t):
        even, odd = spots[0, 2 * t], spots[0, 2 * t + 1]
        values = buf[t]
        new_even = acc[even] + values
        new_odd = acc[odd] + values
        pltpu.store(acc.at[even], new_even, mask=left)
        pltpu.store(acc.at[odd], new_odd, mask=jnp.logical_not(left))

    @pl.loop(0, live_chunks)
    def _(index):
        chunk_copy(index).wait()

        @pl.loop(0, chunk // 4)
        def _(t):
            for u in range(4):
                add_pair(index * chunk + t * 4 + u)


def split(x):
    high = x.astype(jnp.bfloat16)
    return high, (x - high.astype(jnp.float32)).astype(jnp.bfloat16)


def fold(acc, in_pairs, highs, lows):
    blocks = acc.shape[0] // 2
    group = 2 * BLOCKS_DEV

    @pl.loop(0, blocks // in_pairs // group)
    def _(chip):
        for inner in range(group):
            away, k = inner // BLOCKS_DEV, inner % BLOCKS_DEV
            at = pl.multiple_of(chip * ROWS_DEV + k * TILE, TILE)
            for jp in range(in_pairs):
                block = (chip * group + inner) * in_pairs + jp
                high, low = split(acc[block] + pltpu.roll(acc[blocks + block], TILE, 1))
                highs[away, pl.ds(at, TILE), jp * LANES:(jp + 1) * LANES] = high
                lows[away, pl.ds(at, TILE), jp * LANES:(jp + 1) * LANES] = low


def first_kernel(out_blocks, in_pairs, chain, counts, seeds, coords, tiles, keep, send,
                 buf, coord_buf, spots, sems, acc, highs, lows, states):
    cols = out_blocks // BLOCKS_DEV
    block = seeds[...] // ROWS_DEV
    target = ((block // cols) ^ lax.axis_index("row")) * ROWS_DEV + seeds[...] % ROWS_DEV
    target = jnp.where(block % cols == lax.axis_index("col"), target, -1)
    entity = lax.broadcasted_iota(jnp.int32, states.shape, 0)
    states[...] = (entity == target).astype(jnp.float32).astype(jnp.bfloat16)
    place_tiles(0, in_pairs, chain, counts, coords, tiles, buf, coord_buf, spots, sems, acc)
    fold(acc, in_pairs, highs, lows)
    for away, out in ((1, send), (0, keep)):
        out[...] = jnp.dot(highs[away], states[...], preferred_element_type=jnp.float32) + jnp.dot(
            lows[away], states[...], preferred_element_type=jnp.float32)


def dense_kernel(step, in_pairs, chain, counts, coords, tiles, highs, lows,
                 buf, coord_buf, spots, sems, acc):
    place_tiles(step, in_pairs, chain, counts, coords, tiles, buf, coord_buf, spots, sems, acc)
    fold(acc, in_pairs, highs, lows)


def product_kernel(parts, highs, lows, *refs):
    pieces, (keep, send, weights) = refs[:parts], refs[parts:]
    for k, piece in enumerate(pieces):
        high, low = split(piece[...])
        weights[k * ROWS_DEV:(k + 1) * ROWS_DEV, :QUERIES] = high
        weights[k * ROWS_DEV:(k + 1) * ROWS_DEV, QUERIES:] = low
    for away, out in ((1, send), (0, keep)):
        both = jnp.dot(highs[away], weights[...], preferred_element_type=jnp.float32)
        rest = jnp.dot(lows[away], weights[:, :QUERIES], preferred_element_type=jnp.float32)
        out[...] = both[:, :QUERIES] + (both[:, QUERIES:] + rest)


def shards(tiles, tile_coords, tile_count, seeds, chain):
    row_total = lax.axis_size("row")
    col_total = lax.axis_size("col")
    out_blocks = col_total * BLOCKS_DEV
    in_pairs = row_total
    depth_total = col_total // 2
    rows_out = depth_total * ROWS_DEV
    rows_in = in_pairs * LANES
    relations, pairs = tiles.shape[2], tiles.shape[3]
    f32, bf16 = jnp.float32, jnp.bfloat16

    tiles = tiles.reshape(relations, pairs, TILE, 2 * TILE)
    coords = tile_coords.reshape(relations, 2, 2 * pairs)
    seeds = seeds[None, :]

    smem = pl.BlockSpec(memory_space=pltpu.SMEM)
    vmem = pl.BlockSpec(memory_space=pltpu.VMEM)
    hbm = pl.BlockSpec(memory_space=pltpu.HBM)
    dense_bytes = out_blocks * in_pairs * TILE * LANES * 4
    dense_params = pltpu.CompilerParams(vmem_limit_bytes=2 * dense_bytes + pairs * TILE * LANES * 4 + (2 << 20))
    first_params = pltpu.CompilerParams(vmem_limit_bytes=3 * dense_bytes + pairs * TILE * LANES * 4 + (4 << 20))
    product_params = pltpu.CompilerParams(vmem_limit_bytes=rows_in * rows_out + (8 << 20))
    work = [
        pltpu.VMEM((pairs, TILE, 2 * TILE), f32),
        pltpu.VMEM((2, 2 * pairs), jnp.int32),
        pltpu.SMEM((1, 2 * pairs), jnp.int32),
        pltpu.SemaphoreType.DMA((MIN_SHARE + 1,)),
        pltpu.VMEM((2 * out_blocks * in_pairs, TILE, LANES), f32),
    ]
    dense = pltpu.VMEM((2, rows_out, rows_in), bf16)
    partial = pltpu.VMEM((rows_out, QUERIES), f32)

    def local(x):
        return pltpu.with_memory_space_constraint(x, pltpu.VMEM)

    def remain(x):
        return pltpu.with_memory_space_constraint(x, pltpu.HBM)

    given = [remain(x) for x in (chain, tile_count, seeds, coords, tiles)]

    def first():
        return pl.pallas_call(
            functools.partial(first_kernel, out_blocks, in_pairs),
            out_shape=[partial, partial],
            in_specs=[smem, smem, vmem, hbm, hbm],
            out_specs=[vmem, vmem],
            scratch_shapes=work + [pltpu.VMEM(dense.shape, bf16)] * 2 + [pltpu.VMEM((rows_in, QUERIES), bf16)],
            compiler_params=first_params,
            name="first",
        )(*given)

    def densify(step):
        return pl.pallas_call(
            functools.partial(dense_kernel, step, in_pairs),
            out_shape=[dense, dense],
            in_specs=[smem, smem, hbm, hbm],
            out_specs=[vmem, vmem],
            scratch_shapes=work,
            compiler_params=dense_params,
            cost_estimate=pl.CostEstimate(flops=0, bytes_accessed=8 << 20, transcendentals=0),
        )(*given[:2], *given[3:])

    def product(highs, lows, pieces):
        return pl.pallas_call(
            functools.partial(product_kernel, len(pieces)),
            out_shape=[partial, partial],
            in_specs=[vmem] * (2 + len(pieces)),
            out_specs=[vmem, vmem],
            scratch_shapes=[pltpu.VMEM((rows_in, 2 * QUERIES), bf16)],
            compiler_params=product_params,
            name="product",
        )(local(highs), local(lows), *map(local, pieces))

    def swap(x, axis, size, flip):
        return lax.ppermute(x, axis, [(i, i ^ flip) for i in range(size)])

    keep, send = first()
    for step in range(HOPS):
        summed = keep + swap(send, "col", col_total, 1)
        arrived = [
            swap(summed[k * ROWS_DEV:(k + 1) * ROWS_DEV], "col", col_total, 2 * k)
            for k in range(1, depth_total)
        ]
        if step + 1 < HOPS:
            highs, lows = densify(step + 1)
        owned = summed[:ROWS_DEV]
        for part in arrived:
            owned = owned + part
        if step + 1 < HOPS:
            pieces = [owned] + [swap(owned, "row", row_total, k) for k in range(1, row_total)]
            keep, send = product(highs, lows, pieces)

    squares = jnp.sum(owned * owned, axis=0, keepdims=True)
    devices = row_total * col_total
    shared = lax.all_to_all(
        jnp.broadcast_to(squares, (devices, QUERIES)), ("row", "col"), 0, 0, tiled=True)
    totals = jnp.sum(shared, axis=0)
    return owned * lax.rsqrt(totals / (devices * ROWS_DEV) + 1e-06)


def solution(mesh):
    in_specs = (
        P("row", "col", None, None, None, None),
        P("row", "col", None, None, None),
        P("row", "col", None),
        P(),
        P(),
    )
    out_specs = P(("row", "col"), None)
    return jax.shard_map(shards, mesh=mesh, in_specs=in_specs, out_specs=out_specs, check_vma=False)
```

```python
import functools

import jax
import jax.numpy as jnp
from jax import lax
from jax.experimental import pallas as pl
from jax.experimental.pallas import tpu as pltpu
from jax.sharding import PartitionSpec as P


QUERIES = 128
TILE = 64
BLOCKS_DEV = 2
HOPS = 3
ROWS_DEV = BLOCKS_DEV * TILE
LANES = 128
MIN_SHARE = 8


def place_tiles(step, in_pairs, chain, counts, coords, tiles, buf, coord_buf, spots, sems, acc):
    pairs = tiles.shape[1]
    chunk = pairs // MIN_SHARE
    blocks = acc.shape[0] // 2
    relation = chain[step]
    live_chunks = counts[0, 0, relation] // (2 * chunk)
    copy_coords = pltpu.make_async_copy(coords.at[relation], coord_buf, sems.at[MIN_SHARE])
    copy_coords.start()

    def chunk_copy(index):
        span = pl.ds(index * chunk, chunk)
        return pltpu.make_async_copy(tiles.at[relation, span], buf.at[span], sems.at[index])

    for index in range(MIN_SHARE):
        @pl.when(index < live_chunks)
        def _(index=index):
            chunk_copy(index).start()

    copy_coords.wait()
    slot = lax.broadcasted_iota(jnp.int32, (1, 2 * pairs), 1)
    i = coord_buf[0:1, :] ^ (lax.axis_index("col") * BLOCKS_DEV)
    j = coord_buf[1:2, :] ^ (lax.axis_index("row") * BLOCKS_DEV)
    coord_buf[0:1, :] = ((j ^ slot) & 1) * blocks + i * in_pairs + (j >> 1)
    copy_spots = pltpu.make_async_copy(coord_buf.at[pl.ds(0, 1)], spots, sems.at[MIN_SHARE])
    copy_spots.start()

    @pl.loop(0, 2 * blocks // 8)
    def _(b):
        for u in range(8):
            acc[b * 8 + u] = jnp.zeros((TILE, LANES), jnp.float32)

    left = lax.broadcasted_iota(jnp.int32, (TILE, LANES), 1) < TILE
    copy_spots.wait()

    def add_pair(t):
        even, odd = spots[0, 2 * t], spots[0, 2 * t + 1]
        values = buf[t]
        new_even = acc[even] + values
        new_odd = acc[odd] + values
        pltpu.store(acc.at[even], new_even, mask=left)
        pltpu.store(acc.at[odd], new_odd, mask=jnp.logical_not(left))

    @pl.loop(0, live_chunks)
    def _(index):
        chunk_copy(index).wait()

        @pl.loop(0, chunk // 4)
        def _(t):
            for u in range(4):
                add_pair(index * chunk + t * 4 + u)


def split(x):
    high = x.astype(jnp.bfloat16)
    return high, (x - high.astype(jnp.float32)).astype(jnp.bfloat16)


def block_rows(acc, in_pairs, first, high, low, at):
    blocks = acc.shape[0] // 2
    for k in range(BLOCKS_DEV):
        for jp in range(in_pairs):
            block = (first + k) * in_pairs + jp
            span = (pl.ds(at + k * TILE, TILE), pl.ds(jp * LANES, LANES))
            high[span], low[span] = split(acc[block] + pltpu.roll(acc[blocks + block], TILE, 1))


def one_hot_product(acc, states, in_pairs, away, high, low, out):
    for chip in range(out.shape[0] // ROWS_DEV):
        span = pl.ds(chip * ROWS_DEV, ROWS_DEV)
        block_rows(acc, in_pairs, (2 * chip + away) * BLOCKS_DEV, high, low, chip * ROWS_DEV)
        out[span] = jnp.dot(high[span], states[...], preferred_element_type=jnp.float32) + jnp.dot(
            low[span], states[...], preferred_element_type=jnp.float32)


def first_send_kernel(in_pairs, chain, counts, seeds, coords, tiles, send, acc, states,
                      buf, coord_buf, spots, sems, high, low):
    cols = send.shape[0] // ROWS_DEV * 2
    block = seeds[...] // ROWS_DEV
    target = ((block // cols) ^ lax.axis_index("row")) * ROWS_DEV + seeds[...] % ROWS_DEV
    target = jnp.where(block % cols == lax.axis_index("col"), target, -1)
    entity = lax.broadcasted_iota(jnp.int32, states.shape, 0)
    states[...] = (entity == target).astype(jnp.float32).astype(jnp.bfloat16)
    place_tiles(0, in_pairs, chain, counts, coords, tiles, buf, coord_buf, spots, sems, acc)
    one_hot_product(acc, states, in_pairs, 1, high, low, send)


def first_keep_kernel(in_pairs, acc, states, keep, high, low):
    one_hot_product(acc, states, in_pairs, 0, high, low, keep)


def dense_kernel(step, in_pairs, chain, counts, coords, tiles, keep_high, keep_low, send_high, send_low,
                 buf, coord_buf, spots, sems, acc):
    place_tiles(step, in_pairs, chain, counts, coords, tiles, buf, coord_buf, spots, sems, acc)

    @pl.loop(0, keep_high.shape[0] // ROWS_DEV)
    def _(chip):
        at = pl.multiple_of(chip * ROWS_DEV, ROWS_DEV)
        block_rows(acc, in_pairs, 2 * chip * BLOCKS_DEV, keep_high, keep_low, at)
        block_rows(acc, in_pairs, (2 * chip + 1) * BLOCKS_DEV, send_high, send_low, at)


def product_kernel(parts, high, low, *refs):
    pieces, (out, weights) = refs[:parts], refs[parts:]
    for k, piece in enumerate(pieces):
        above, below = split(piece[...])
        weights[k * ROWS_DEV:(k + 1) * ROWS_DEV, :QUERIES] = above
        weights[k * ROWS_DEV:(k + 1) * ROWS_DEV, QUERIES:] = below
    both = jnp.dot(high[...], weights[...], preferred_element_type=jnp.float32)
    rest = jnp.dot(low[...], weights[:, :QUERIES], preferred_element_type=jnp.float32)
    out[...] = both[:, :QUERIES] + (both[:, QUERIES:] + rest)


def shards(tiles, tile_coords, tile_count, seeds, chain):
    row_total = lax.axis_size("row")
    col_total = lax.axis_size("col")
    out_blocks = col_total * BLOCKS_DEV
    in_pairs = row_total
    depth_total = col_total // 2
    rows_out = depth_total * ROWS_DEV
    rows_in = in_pairs * LANES
    relations, pairs = tiles.shape[2], tiles.shape[3]
    f32, bf16 = jnp.float32, jnp.bfloat16

    tiles = tiles.reshape(relations, pairs, TILE, 2 * TILE)
    coords = tile_coords.reshape(relations, 2, 2 * pairs)
    seeds = seeds[None, :]

    smem = pl.BlockSpec(memory_space=pltpu.SMEM)
    vmem = pl.BlockSpec(memory_space=pltpu.VMEM)
    hbm = pl.BlockSpec(memory_space=pltpu.HBM)
    dense_bytes = out_blocks * in_pairs * TILE * LANES * 4
    tile_bytes = pairs * TILE * LANES * 4
    work = [
        pltpu.VMEM((pairs, TILE, 2 * TILE), f32),
        pltpu.VMEM((2, 2 * pairs), jnp.int32),
        pltpu.SMEM((1, 2 * pairs), jnp.int32),
        pltpu.SemaphoreType.DMA((MIN_SHARE + 1,)),
    ]
    sums = pltpu.VMEM((2 * out_blocks * in_pairs, TILE, LANES), f32)
    half = pltpu.VMEM((rows_out, rows_in), bf16)
    partial = pltpu.VMEM((rows_out, QUERIES), f32)
    one_hot = pltpu.VMEM((rows_in, QUERIES), bf16)

    def limit(size):
        return pltpu.CompilerParams(vmem_limit_bytes=size + (2 << 20))

    def cost(flops):
        return pl.CostEstimate(flops=flops, bytes_accessed=1 << 20, transcendentals=0)

    def local(x):
        return pltpu.with_memory_space_constraint(x, pltpu.VMEM)

    def remain(x):
        return pltpu.with_memory_space_constraint(x, pltpu.HBM)

    given = [remain(x) for x in (chain, tile_count, seeds, coords, tiles)]

    def first_send():
        return pl.pallas_call(
            functools.partial(first_send_kernel, in_pairs),
            out_shape=[partial, sums, one_hot],
            in_specs=[smem, smem, vmem, hbm, hbm],
            out_specs=[vmem] * 3,
            scratch_shapes=work + [half] * 2,
            compiler_params=limit(tile_bytes + dense_bytes // 2),
            name="first_send",
        )(*given)

    def first_keep(acc, states):
        return pl.pallas_call(
            functools.partial(first_keep_kernel, in_pairs),
            out_shape=partial,
            in_specs=[vmem] * 2,
            out_specs=vmem,
            scratch_shapes=[half] * 2,
            compiler_params=limit(dense_bytes // 2),
            cost_estimate=cost(4 * rows_out * rows_in * QUERIES),
            name="first_keep",
        )(local(acc), local(states))

    def densify(step):
        return pl.pallas_call(
            functools.partial(dense_kernel, step, in_pairs),
            out_shape=[half] * 4,
            in_specs=[smem, smem, hbm, hbm],
            out_specs=[vmem] * 4,
            scratch_shapes=work + [sums],
            compiler_params=limit(tile_bytes + 2 * dense_bytes),
            cost_estimate=pl.CostEstimate(flops=0, bytes_accessed=8 << 20, transcendentals=0),
        )(*given[:2], *given[3:])

    def product(high, low, pieces):
        return pl.pallas_call(
            functools.partial(product_kernel, len(pieces)),
            out_shape=partial,
            in_specs=[vmem] * (2 + len(pieces)),
            out_specs=vmem,
            scratch_shapes=[pltpu.VMEM((rows_in, 2 * QUERIES), bf16)],
            compiler_params=limit(4 << 20),
            cost_estimate=cost(6 * rows_out * rows_in * QUERIES),
            name="product",
        )(local(high), local(low), *map(local, pieces))

    def swap(x, axis, size, flip):
        return lax.ppermute(x, axis, [(i, i ^ flip) for i in range(size)])

    for step in range(HOPS):
        if step == 0:
            send, acc, states = first_send()
        else:
            send = product(*relation[2:], pieces)
        crossing = swap(send, "col", col_total, 1)
        keep = first_keep(acc, states) if step == 0 else product(*relation[:2], pieces)
        summed = keep + crossing
        arrived = [
            swap(summed[k * ROWS_DEV:(k + 1) * ROWS_DEV], "col", col_total, 2 * k)
            for k in range(1, depth_total)
        ]
        if step + 1 < HOPS:
            relation = densify(step + 1)
        owned = summed[:ROWS_DEV]
        for part in arrived:
            owned = owned + part
        if step + 1 < HOPS:
            pieces = [owned] + [swap(owned, "row", row_total, k) for k in range(1, row_total)]

    squares = jnp.sum(owned * owned, axis=0, keepdims=True)
    devices = row_total * col_total
    shared = lax.all_to_all(
        jnp.broadcast_to(squares, (devices, QUERIES)), ("row", "col"), 0, 0, tiled=True)
    totals = jnp.sum(shared, axis=0)
    return owned * lax.rsqrt(totals / (devices * ROWS_DEV) + 1e-06)


def solution(mesh):
    in_specs = (
        P("row", "col", None, None, None, None),
        P("row", "col", None, None, None),
        P("row", "col", None),
        P(),
        P(),
    )
    out_specs = P(("row", "col"), None)
    return jax.shard_map(shards, mesh=mesh, in_specs=in_specs, out_specs=out_specs, check_vma=False)
```

```python
import functools

import jax
import jax.numpy as jnp
from jax import lax
from jax.experimental import pallas as pl
from jax.experimental.pallas import tpu as pltpu
from jax.sharding import PartitionSpec as P


QUERIES = 128
TILE = 64
BLOCKS_DEV = 2
HOPS = 3
ROWS_DEV = BLOCKS_DEV * TILE
LANES = 128
MIN_SHARE = 8


def visits(chips):
    return [0, *range(2, chips), 1], [0, 2, 1, *range(3, chips)]


def place_tiles(step, in_pairs, chain, counts, coords, tiles, buf, coord_buf, spots, sems, acc):
    pairs = tiles.shape[1]
    chunk = pairs // MIN_SHARE
    blocks = acc.shape[0] // 2
    relation = chain[step]
    live_chunks = counts[0, 0, relation] // (2 * chunk)
    copy_coords = pltpu.make_async_copy(coords.at[relation], coord_buf, sems.at[MIN_SHARE])
    copy_coords.start()

    def chunk_copy(index):
        span = pl.ds(index * chunk, chunk)
        return pltpu.make_async_copy(tiles.at[relation, span], buf.at[span], sems.at[index])

    for index in range(MIN_SHARE):
        @pl.when(index < live_chunks)
        def _(index=index):
            chunk_copy(index).start()

    copy_coords.wait()
    slot = lax.broadcasted_iota(jnp.int32, (1, 2 * pairs), 1)
    i = coord_buf[0:1, :] ^ (lax.axis_index("col") * BLOCKS_DEV)
    group = 2 * BLOCKS_DEV
    owner = (lax.axis_index("col") ^ (i // BLOCKS_DEV)) & 1
    chip = i // group
    turn = jnp.zeros_like(i)
    for core, order in enumerate(visits(blocks // in_pairs // group)):
        for place, flip in enumerate(order):
            turn = jnp.where((owner == core) & (chip == flip), place, turn)
    i = turn * group + i % group
    j = coord_buf[1:2, :] ^ (lax.axis_index("row") * BLOCKS_DEV)
    coord_buf[0:1, :] = ((j ^ slot) & 1) * blocks + i * in_pairs + (j >> 1)
    copy_spots = pltpu.make_async_copy(coord_buf.at[pl.ds(0, 1)], spots, sems.at[MIN_SHARE])
    copy_spots.start()

    @pl.loop(0, 2 * blocks // 8)
    def _(b):
        for u in range(8):
            acc[b * 8 + u] = jnp.zeros((TILE, LANES), jnp.float32)

    left = lax.broadcasted_iota(jnp.int32, (TILE, LANES), 1) < TILE
    copy_spots.wait()

    def add_pair(t):
        even, odd = spots[0, 2 * t], spots[0, 2 * t + 1]
        values = buf[t]
        new_even = acc[even] + values
        new_odd = acc[odd] + values
        pltpu.store(acc.at[even], new_even, mask=left)
        pltpu.store(acc.at[odd], new_odd, mask=jnp.logical_not(left))

    @pl.loop(0, live_chunks)
    def _(index):
        chunk_copy(index).wait()

        @pl.loop(0, chunk // 4)
        def _(t):
            for u in range(4):
                add_pair(index * chunk + t * 4 + u)


def split(x):
    high = x.astype(jnp.bfloat16)
    return high, (x - high.astype(jnp.float32)).astype(jnp.bfloat16)


def block_rows(acc, in_pairs, first, high, low, at):
    blocks = acc.shape[0] // 2
    for k in range(BLOCKS_DEV):
        for jp in range(in_pairs):
            block = (first + k) * in_pairs + jp
            span = (pl.ds(at + k * TILE, TILE), pl.ds(jp * LANES, LANES))
            high[span], low[span] = split(acc[block] + pltpu.roll(acc[blocks + block], TILE, 1))


def one_hot_product(acc, states, in_pairs, away, high, low, out):
    for chip in range(out.shape[0] // ROWS_DEV):
        span = pl.ds(chip * ROWS_DEV, ROWS_DEV)
        block_rows(acc, in_pairs, (2 * chip + away) * BLOCKS_DEV, high, low, chip * ROWS_DEV)
        out[span] = jnp.dot(high[span], states[...], preferred_element_type=jnp.float32) + jnp.dot(
            low[span], states[...], preferred_element_type=jnp.float32)


def first_send_kernel(in_pairs, chain, counts, seeds, coords, tiles, send, acc, states,
                      buf, coord_buf, spots, sems, high, low):
    cols = send.shape[0] // ROWS_DEV * 2
    block = seeds[...] // ROWS_DEV
    target = ((block // cols) ^ lax.axis_index("row")) * ROWS_DEV + seeds[...] % ROWS_DEV
    target = jnp.where(block % cols == lax.axis_index("col"), target, -1)
    entity = lax.broadcasted_iota(jnp.int32, states.shape, 0)
    states[...] = (entity == target).astype(jnp.float32).astype(jnp.bfloat16)
    place_tiles(0, in_pairs, chain, counts, coords, tiles, buf, coord_buf, spots, sems, acc)
    one_hot_product(acc, states, in_pairs, 1, high, low, send)


def first_keep_kernel(in_pairs, acc, states, keep, high, low):
    one_hot_product(acc, states, in_pairs, 0, high, low, keep)


def dense_kernel(step, in_pairs, chain, counts, coords, tiles, keep_high, keep_low, send_high, send_low,
                 buf, coord_buf, spots, sems, acc):
    place_tiles(step, in_pairs, chain, counts, coords, tiles, buf, coord_buf, spots, sems, acc)

    @pl.loop(0, keep_high.shape[0] // ROWS_DEV)
    def _(chip):
        at = pl.multiple_of(chip * ROWS_DEV, ROWS_DEV)
        block_rows(acc, in_pairs, 2 * chip * BLOCKS_DEV, keep_high, keep_low, at)
        block_rows(acc, in_pairs, (2 * chip + 1) * BLOCKS_DEV, send_high, send_low, at)


def product_kernel(parts, high, low, *refs):
    pieces, (out, weights) = refs[:parts], refs[parts:]
    for k, piece in enumerate(pieces):
        above, below = split(piece[...])
        weights[k * ROWS_DEV:(k + 1) * ROWS_DEV, :QUERIES] = above
        weights[k * ROWS_DEV:(k + 1) * ROWS_DEV, QUERIES:] = below
    both = jnp.dot(high[...], weights[...], preferred_element_type=jnp.float32)
    rest = jnp.dot(low[...], weights[:, :QUERIES], preferred_element_type=jnp.float32)
    out[...] = both[:, :QUERIES] + (both[:, QUERIES:] + rest)


def shards(tiles, tile_coords, tile_count, seeds, chain):
    row_total = lax.axis_size("row")
    col_total = lax.axis_size("col")
    out_blocks = col_total * BLOCKS_DEV
    in_pairs = row_total
    depth_total = col_total // 2
    rows_out = depth_total * ROWS_DEV
    rows_in = in_pairs * LANES
    relations, pairs = tiles.shape[2], tiles.shape[3]
    f32, bf16 = jnp.float32, jnp.bfloat16

    tiles = tiles.reshape(relations, pairs, TILE, 2 * TILE)
    coords = tile_coords.reshape(relations, 2, 2 * pairs)
    seeds = seeds[None, :]

    smem = pl.BlockSpec(memory_space=pltpu.SMEM)
    vmem = pl.BlockSpec(memory_space=pltpu.VMEM)
    hbm = pl.BlockSpec(memory_space=pltpu.HBM)
    dense_bytes = out_blocks * in_pairs * TILE * LANES * 4
    tile_bytes = pairs * TILE * LANES * 4
    work = [
        pltpu.VMEM((pairs, TILE, 2 * TILE), f32),
        pltpu.VMEM((2, 2 * pairs), jnp.int32),
        pltpu.SMEM((1, 2 * pairs), jnp.int32),
        pltpu.SemaphoreType.DMA((MIN_SHARE + 1,)),
    ]
    sums = pltpu.VMEM((2 * out_blocks * in_pairs, TILE, LANES), f32)
    half = pltpu.VMEM((rows_out, rows_in), bf16)
    partial = pltpu.VMEM((rows_out, QUERIES), f32)
    one_hot = pltpu.VMEM((rows_in, QUERIES), bf16)

    def limit(size):
        return pltpu.CompilerParams(vmem_limit_bytes=size + (2 << 20))

    def cost(flops):
        return pl.CostEstimate(flops=flops, bytes_accessed=1 << 20, transcendentals=0)

    def local(x):
        return pltpu.with_memory_space_constraint(x, pltpu.VMEM)

    def remain(x):
        return pltpu.with_memory_space_constraint(x, pltpu.HBM)

    given = [remain(x) for x in (chain, tile_count, seeds, coords, tiles)]

    def first_send():
        return pl.pallas_call(
            functools.partial(first_send_kernel, in_pairs),
            out_shape=[partial, sums, one_hot],
            in_specs=[smem, smem, vmem, hbm, hbm],
            out_specs=[vmem] * 3,
            scratch_shapes=work + [half] * 2,
            compiler_params=limit(tile_bytes + dense_bytes // 2),
            name="first_send",
        )(*given)

    def first_keep(acc, states):
        return pl.pallas_call(
            functools.partial(first_keep_kernel, in_pairs),
            out_shape=partial,
            in_specs=[vmem] * 2,
            out_specs=vmem,
            scratch_shapes=[half] * 2,
            compiler_params=limit(dense_bytes // 2),
            cost_estimate=cost(4 * rows_out * rows_in * QUERIES),
            name="first_keep",
        )(local(acc), local(states))

    def densify(step):
        return pl.pallas_call(
            functools.partial(dense_kernel, step, in_pairs),
            out_shape=[half] * 4,
            in_specs=[smem, smem, hbm, hbm],
            out_specs=[vmem] * 4,
            scratch_shapes=work + [sums],
            compiler_params=limit(tile_bytes + 2 * dense_bytes),
            cost_estimate=pl.CostEstimate(flops=0, bytes_accessed=8 << 20, transcendentals=0),
        )(*given[:2], *given[3:])

    def product(high, low, pieces):
        return pl.pallas_call(
            functools.partial(product_kernel, len(pieces)),
            out_shape=partial,
            in_specs=[vmem] * (2 + len(pieces)),
            out_specs=vmem,
            scratch_shapes=[pltpu.VMEM((rows_in, 2 * QUERIES), bf16)],
            compiler_params=limit(4 << 20),
            cost_estimate=cost(6 * rows_out * rows_in * QUERIES),
            name="product",
        )(local(high), local(low), *map(local, pieces))

    def swap(x, axis, size, flip):
        return lax.ppermute(x, axis, [(i, i ^ flip) for i in range(size)])

    for step in range(HOPS):
        if step == 0:
            send, acc, states = first_send()
        else:
            send = product(*relation[2:], pieces)
        crossing = swap(send, "col", col_total, 1)
        keep = first_keep(acc, states) if step == 0 else product(*relation[:2], pieces)
        summed = keep + crossing
        arrived = []
        for turn, flips in enumerate(zip(*visits(depth_total))):
            if turn:
                pairs_there = [(2 * z + core, 2 * (z ^ flips[core]) + core)
                               for z in range(depth_total) for core in range(2)]
                arrived.append(
                    lax.ppermute(summed[turn * ROWS_DEV:(turn + 1) * ROWS_DEV], "col", pairs_there))
        if step + 1 < HOPS:
            relation = densify(step + 1)
        owned = summed[:ROWS_DEV]
        for part in arrived:
            owned = owned + part
        if step + 1 < HOPS:
            pieces = [owned] + [swap(owned, "row", row_total, k) for k in range(1, row_total)]

    squares = jnp.sum(owned * owned, axis=0, keepdims=True)
    devices = row_total * col_total
    shared = lax.all_to_all(
        jnp.broadcast_to(squares, (devices, QUERIES)), ("row", "col"), 0, 0, tiled=True)
    totals = jnp.sum(shared, axis=0)
    return owned * lax.rsqrt(totals / (devices * ROWS_DEV) + 1e-06)


def solution(mesh):
    in_specs = (
        P("row", "col", None, None, None, None),
        P("row", "col", None, None, None),
        P("row", "col", None),
        P(),
        P(),
    )
    out_specs = P(("row", "col"), None)
    return jax.shard_map(shards, mesh=mesh, in_specs=in_specs, out_specs=out_specs, check_vma=False)
```

```python
import functools

import jax
import jax.numpy as jnp
from jax import lax
from jax.experimental import pallas as pl
from jax.experimental.pallas import tpu as pltpu
from jax.sharding import PartitionSpec as P


QUERIES = 128
TILE = 64
BLOCKS_DEV = 2
HOPS = 3
ROWS_DEV = BLOCKS_DEV * TILE
LANES = 128
MIN_SHARE = 8


def visits(chips):
    return [*range(2, chips), 1, 0], [2, 1, *range(3, chips), 0]


def place_tiles(step, in_pairs, chain, counts, coords, tiles, buf, coord_buf, spots, sems, acc):
    pairs = tiles.shape[1]
    chunk = pairs // MIN_SHARE
    blocks = acc.shape[0] // 2
    relation = chain[step]
    live_chunks = counts[0, 0, relation] // (2 * chunk)
    copy_coords = pltpu.make_async_copy(coords.at[relation], coord_buf, sems.at[MIN_SHARE])
    copy_coords.start()

    def chunk_copy(index):
        span = pl.ds(index * chunk, chunk)
        return pltpu.make_async_copy(tiles.at[relation, span], buf.at[span], sems.at[index])

    for index in range(MIN_SHARE):
        @pl.when(index < live_chunks)
        def _(index=index):
            chunk_copy(index).start()

    copy_coords.wait()
    slot = lax.broadcasted_iota(jnp.int32, (1, 2 * pairs), 1)
    i = coord_buf[0:1, :] ^ (lax.axis_index("col") * BLOCKS_DEV)
    group = 2 * BLOCKS_DEV
    owner = (lax.axis_index("col") ^ (i // BLOCKS_DEV)) & 1
    chip = i // group
    turn = jnp.zeros_like(i)
    for core, order in enumerate(visits(blocks // in_pairs // group)):
        for place, flip in enumerate(order):
            turn = jnp.where((owner == core) & (chip == flip), place, turn)
    i = turn * group + i % group
    j = coord_buf[1:2, :] ^ (lax.axis_index("row") * BLOCKS_DEV)
    coord_buf[0:1, :] = ((j ^ slot) & 1) * blocks + i * in_pairs + (j >> 1)
    copy_spots = pltpu.make_async_copy(coord_buf.at[pl.ds(0, 1)], spots, sems.at[MIN_SHARE])
    copy_spots.start()

    @pl.loop(0, 2 * blocks // 8)
    def _(b):
        for u in range(8):
            acc[b * 8 + u] = jnp.zeros((TILE, LANES), jnp.float32)

    left = lax.broadcasted_iota(jnp.int32, (TILE, LANES), 1) < TILE
    copy_spots.wait()

    def add_pair(t):
        even, odd = spots[0, 2 * t], spots[0, 2 * t + 1]
        values = buf[t]
        new_even = acc[even] + values
        new_odd = acc[odd] + values
        pltpu.store(acc.at[even], new_even, mask=left)
        pltpu.store(acc.at[odd], new_odd, mask=jnp.logical_not(left))

    @pl.loop(0, live_chunks)
    def _(index):
        chunk_copy(index).wait()

        @pl.loop(0, chunk // 4)
        def _(t):
            for u in range(4):
                add_pair(index * chunk + t * 4 + u)


def split(x):
    high = x.astype(jnp.bfloat16)
    return high, (x - high.astype(jnp.float32)).astype(jnp.bfloat16)


def block_rows(acc, in_pairs, first, high, low, at):
    blocks = acc.shape[0] // 2
    for k in range(BLOCKS_DEV):
        for jp in range(in_pairs):
            block = (first + k) * in_pairs + jp
            span = (pl.ds(at + k * TILE, TILE), pl.ds(jp * LANES, LANES))
            high[span], low[span] = split(acc[block] + pltpu.roll(acc[blocks + block], TILE, 1))


def one_hot_product(acc, states, in_pairs, turn, away, high, low, out):
    for n in range(out.shape[0] // ROWS_DEV):
        span = pl.ds(n * ROWS_DEV, ROWS_DEV)
        block_rows(acc, in_pairs, (2 * (turn + n) + away) * BLOCKS_DEV, high, low, n * ROWS_DEV)
        out[span] = jnp.dot(high[span], states[...], preferred_element_type=jnp.float32) + jnp.dot(
            low[span], states[...], preferred_element_type=jnp.float32)


def first_kernel(in_pairs, cols, chain, counts, seeds, coords, tiles, send, acc, states,
                 buf, coord_buf, spots, sems, high, low):
    block = seeds[...] // ROWS_DEV
    target = ((block // cols) ^ lax.axis_index("row")) * ROWS_DEV + seeds[...] % ROWS_DEV
    target = jnp.where(block % cols == lax.axis_index("col"), target, -1)
    entity = lax.broadcasted_iota(jnp.int32, states.shape, 0)
    states[...] = (entity == target).astype(jnp.float32).astype(jnp.bfloat16)
    place_tiles(0, in_pairs, chain, counts, coords, tiles, buf, coord_buf, spots, sems, acc)
    one_hot_product(acc, states, in_pairs, 0, 1, high, low, send)


def one_hot_kernel(in_pairs, turn, away, acc, states, out, high, low):
    one_hot_product(acc, states, in_pairs, turn, away, high, low, out)


def dense_kernel(step, in_pairs, chain, counts, coords, tiles, keep_high, keep_low, send_high, send_low,
                 buf, coord_buf, spots, sems, acc):
    place_tiles(step, in_pairs, chain, counts, coords, tiles, buf, coord_buf, spots, sems, acc)

    @pl.loop(0, keep_high.shape[0] // ROWS_DEV)
    def _(chip):
        at = pl.multiple_of(chip * ROWS_DEV, ROWS_DEV)
        block_rows(acc, in_pairs, 2 * chip * BLOCKS_DEV, keep_high, keep_low, at)
        block_rows(acc, in_pairs, (2 * chip + 1) * BLOCKS_DEV, send_high, send_low, at)


def multiply(high, low, weights, start, out):
    span = pl.ds(start, out.shape[0])
    both = jnp.dot(high[span], weights[...], preferred_element_type=jnp.float32)
    rest = jnp.dot(low[span], weights[:, :QUERIES], preferred_element_type=jnp.float32)
    out[...] = both[:, :QUERIES] + (both[:, QUERIES:] + rest)


def leading_kernel(high, low, *refs):
    pieces, (out, weights) = refs[:-2], refs[-2:]
    for k, piece in enumerate(pieces):
        above, below = split(piece[...])
        weights[k * ROWS_DEV:(k + 1) * ROWS_DEV, :QUERIES] = above
        weights[k * ROWS_DEV:(k + 1) * ROWS_DEV, QUERIES:] = below
    multiply(high, low, weights, 0, out)


def product_kernel(start, high, low, weights, out):
    multiply(high, low, weights, start, out)


def shards(tiles, tile_coords, tile_count, seeds, chain):
    row_total = lax.axis_size("row")
    col_total = lax.axis_size("col")
    out_blocks = col_total * BLOCKS_DEV
    in_pairs = row_total
    depth_total = col_total // 2
    rows_out = depth_total * ROWS_DEV
    rows_in = in_pairs * LANES
    relations, pairs = tiles.shape[2], tiles.shape[3]
    f32, bf16 = jnp.float32, jnp.bfloat16

    tiles = tiles.reshape(relations, pairs, TILE, 2 * TILE)
    coords = tile_coords.reshape(relations, 2, 2 * pairs)
    seeds = seeds[None, :]

    smem = pl.BlockSpec(memory_space=pltpu.SMEM)
    vmem = pl.BlockSpec(memory_space=pltpu.VMEM)
    hbm = pl.BlockSpec(memory_space=pltpu.HBM)
    dense_bytes = out_blocks * in_pairs * TILE * LANES * 4
    tile_bytes = pairs * TILE * LANES * 4
    work = [
        pltpu.VMEM((pairs, TILE, 2 * TILE), f32),
        pltpu.VMEM((2, 2 * pairs), jnp.int32),
        pltpu.SMEM((1, 2 * pairs), jnp.int32),
        pltpu.SemaphoreType.DMA((MIN_SHARE + 1,)),
    ]
    sums = pltpu.VMEM((2 * out_blocks * in_pairs, TILE, LANES), f32)
    half = pltpu.VMEM((rows_out, rows_in), bf16)
    lead = pltpu.VMEM((ROWS_DEV, QUERIES), f32)
    rest = pltpu.VMEM((rows_out - ROWS_DEV, QUERIES), f32)
    halved = pltpu.VMEM((rows_in, 2 * QUERIES), bf16)
    one_hot = pltpu.VMEM((rows_in, QUERIES), bf16)

    def limit(size):
        return pltpu.CompilerParams(vmem_limit_bytes=size + (2 << 20))

    def cost(flops):
        return pl.CostEstimate(flops=flops, bytes_accessed=1 << 20, transcendentals=0)

    def local(x):
        return pltpu.with_memory_space_constraint(x, pltpu.VMEM)

    def remain(x):
        return pltpu.with_memory_space_constraint(x, pltpu.HBM)

    given = [remain(x) for x in (chain, tile_count, seeds, coords, tiles)]

    def first():
        return pl.pallas_call(
            functools.partial(first_kernel, in_pairs, col_total),
            out_shape=[lead, sums, one_hot],
            in_specs=[smem, smem, vmem, hbm, hbm],
            out_specs=[vmem] * 3,
            scratch_shapes=work + [pltpu.VMEM((ROWS_DEV, rows_in), bf16)] * 2,
            compiler_params=limit(tile_bytes + dense_bytes // 2),
            name="first",
        )(*given)

    def one_hot_part(acc, states, away, shape):
        turn = 0 if shape is lead else 1
        return pl.pallas_call(
            functools.partial(one_hot_kernel, in_pairs, turn, away),
            out_shape=shape,
            in_specs=[vmem] * 2,
            out_specs=vmem,
            scratch_shapes=[pltpu.VMEM((shape.shape[0], rows_in), bf16)] * 2,
            compiler_params=limit(dense_bytes // 2),
            cost_estimate=cost(4 * shape.shape[0] * rows_in * QUERIES),
            name="one_hot_part",
        )(local(acc), local(states))

    def densify(step):
        return pl.pallas_call(
            functools.partial(dense_kernel, step, in_pairs),
            out_shape=[half] * 4,
            in_specs=[smem, smem, hbm, hbm],
            out_specs=[vmem] * 4,
            scratch_shapes=work + [sums],
            compiler_params=limit(tile_bytes + 2 * dense_bytes),
            cost_estimate=pl.CostEstimate(flops=0, bytes_accessed=8 << 20, transcendentals=0),
        )(*given[:2], *given[3:])

    def leading(high, low, pieces):
        return pl.pallas_call(
            leading_kernel,
            out_shape=[lead, halved],
            in_specs=[vmem] * (2 + len(pieces)),
            out_specs=[vmem] * 2,
            compiler_params=limit(4 << 20),
            cost_estimate=cost(6 * ROWS_DEV * rows_in * QUERIES),
            name="leading",
        )(local(high), local(low), *map(local, pieces))

    def product(high, low, weights, shape):
        return pl.pallas_call(
            functools.partial(product_kernel, 0 if shape is lead else ROWS_DEV),
            out_shape=shape,
            in_specs=[vmem] * 3,
            out_specs=vmem,
            compiler_params=limit(4 << 20),
            cost_estimate=cost(6 * shape.shape[0] * rows_in * QUERIES),
            name="product",
        )(local(high), local(low), local(weights))

    def swap(x, axis, size, flip):
        return lax.ppermute(x, axis, [(i, i ^ flip) for i in range(size)])

    def kept(away, shape):
        if step == 0:
            return one_hot_part(acc, states, away, shape)
        return product(*relation[2 * away:2 * away + 2], weights, shape)

    for step in range(HOPS):
        if step == 0:
            send, acc, states = first()
        else:
            send, weights = leading(*relation[2:], pieces)
        crossing = [swap(send, "col", col_total, 1)]
        send = kept(1, rest)
        crossing.append(swap(send, "col", col_total, 1))
        head = kept(0, lead) + crossing[0]
        tail = kept(0, rest) + crossing[1]
        arrived = []
        for turn, flips in enumerate(zip(*visits(depth_total))):
            part = tail[(turn - 1) * ROWS_DEV:turn * ROWS_DEV] if turn else head
            if turn == depth_total - 1:
                arrived.append(part)
                continue
            there = [(2 * z + core, 2 * (z ^ flips[core]) + core)
                     for z in range(depth_total) for core in range(2)]
            arrived.append(lax.ppermute(part, "col", there))
        if step + 1 < HOPS:
            following = densify(step + 1)
        owned = arrived[-1]
        for part in arrived[:-1]:
            owned = owned + part
        if step + 1 < HOPS:
            relation = following
            pieces = [owned] + [swap(owned, "row", row_total, k) for k in range(1, row_total)]

    squares = jnp.sum(owned * owned, axis=0, keepdims=True)
    devices = row_total * col_total
    shared = lax.all_to_all(
        jnp.broadcast_to(squares, (devices, QUERIES)), ("row", "col"), 0, 0, tiled=True)
    totals = jnp.sum(shared, axis=0)
    return owned * lax.rsqrt(totals / (devices * ROWS_DEV) + 1e-06)


def solution(mesh):
    in_specs = (
        P("row", "col", None, None, None, None),
        P("row", "col", None, None, None),
        P("row", "col", None),
        P(),
        P(),
    )
    out_specs = P(("row", "col"), None)
    return jax.shard_map(shards, mesh=mesh, in_specs=in_specs, out_specs=out_specs, check_vma=False)
```

```python
import functools

import jax
import jax.numpy as jnp
from jax import lax
from jax.experimental import pallas as pl
from jax.experimental.pallas import tpu as pltpu
from jax.sharding import PartitionSpec as P


QUERIES = 128
TILE = 64
BLOCKS_DEV = 2
HOPS = 3
ROWS_DEV = BLOCKS_DEV * TILE
LANES = 128
MIN_SHARE = 8


def visits(chips):
    return [*range(2, chips), 1, 0], [2, 1, *range(3, chips), 0]


def place_tiles(step, in_pairs, chain, counts, coords, tiles, buf, coord_buf, spots, sems, acc):
    pairs = tiles.shape[1]
    chunk = pairs // MIN_SHARE
    blocks = acc.shape[0] // 2
    relation = chain[step]
    live_chunks = counts[0, 0, relation] // (2 * chunk)
    copy_coords = pltpu.make_async_copy(coords.at[relation], coord_buf, sems.at[MIN_SHARE])
    copy_coords.start()

    def chunk_copy(index):
        span = pl.ds(index * chunk, chunk)
        return pltpu.make_async_copy(tiles.at[relation, span], buf.at[span], sems.at[index])

    for index in range(MIN_SHARE):
        @pl.when(index < live_chunks)
        def _(index=index):
            chunk_copy(index).start()

    copy_coords.wait()
    slot = lax.broadcasted_iota(jnp.int32, (1, 2 * pairs), 1)
    i = coord_buf[0:1, :] ^ (lax.axis_index("col") * BLOCKS_DEV)
    group = 2 * BLOCKS_DEV
    owner = (lax.axis_index("col") ^ (i // BLOCKS_DEV)) & 1
    chip = i // group
    turn = jnp.zeros_like(i)
    for core, order in enumerate(visits(blocks // in_pairs // group)):
        for place, flip in enumerate(order):
            turn = jnp.where((owner == core) & (chip == flip), place, turn)
    i = turn * group + i % group
    j = coord_buf[1:2, :] ^ (lax.axis_index("row") * BLOCKS_DEV)
    coord_buf[0:1, :] = ((j ^ slot) & 1) * blocks + i * in_pairs + (j >> 1)
    copy_spots = pltpu.make_async_copy(coord_buf.at[pl.ds(0, 1)], spots, sems.at[MIN_SHARE])
    copy_spots.start()

    @pl.loop(0, 2 * blocks // 8)
    def _(b):
        for u in range(8):
            acc[b * 8 + u] = jnp.zeros((TILE, LANES), jnp.float32)

    left = lax.broadcasted_iota(jnp.int32, (TILE, LANES), 1) < TILE
    copy_spots.wait()

    def add_pair(t):
        even, odd = spots[0, 2 * t], spots[0, 2 * t + 1]
        values = buf[t]
        new_even = acc[even] + values
        new_odd = acc[odd] + values
        pltpu.store(acc.at[even], new_even, mask=left)
        pltpu.store(acc.at[odd], new_odd, mask=jnp.logical_not(left))

    @pl.loop(0, live_chunks)
    def _(index):
        chunk_copy(index).wait()

        @pl.loop(0, chunk // 4)
        def _(t):
            for u in range(4):
                add_pair(index * chunk + t * 4 + u)


def split(x):
    high = x.astype(jnp.bfloat16)
    return high, (x - high.astype(jnp.float32)).astype(jnp.bfloat16)


def block_rows(acc, in_pairs, first, high, low, at):
    blocks = acc.shape[0] // 2
    for k in range(BLOCKS_DEV):
        for jp in range(in_pairs):
            block = (first + k) * in_pairs + jp
            span = (pl.ds(at + k * TILE, TILE), pl.ds(jp * LANES, LANES))
            high[span], low[span] = split(acc[block] + pltpu.roll(acc[blocks + block], TILE, 1))


def one_hot_product(acc, states, in_pairs, turn, away, high, low, out):
    for n in range(out.shape[0] // ROWS_DEV):
        span = pl.ds(n * ROWS_DEV, ROWS_DEV)
        block_rows(acc, in_pairs, (2 * (turn + n) + away) * BLOCKS_DEV, high, low, n * ROWS_DEV)
        out[span] = jnp.dot(high[span], states[...], preferred_element_type=jnp.float32) + jnp.dot(
            low[span], states[...], preferred_element_type=jnp.float32)


def first_kernel(in_pairs, cols, chain, counts, seeds, coords, tiles, send, acc, states,
                 buf, coord_buf, spots, sems, high, low):
    block = seeds[...] // ROWS_DEV
    target = ((block // cols) ^ lax.axis_index("row")) * ROWS_DEV + seeds[...] % ROWS_DEV
    target = jnp.where(block % cols == lax.axis_index("col"), target, -1)
    entity = lax.broadcasted_iota(jnp.int32, states.shape, 0)
    states[...] = (entity == target).astype(jnp.float32).astype(jnp.bfloat16)
    place_tiles(0, in_pairs, chain, counts, coords, tiles, buf, coord_buf, spots, sems, acc)
    one_hot_product(acc, states, in_pairs, 0, 1, high, low, send)


def one_hot_kernel(in_pairs, turn, away, acc, states, out, high, low):
    one_hot_product(acc, states, in_pairs, turn, away, high, low, out)


def dense_kernel(step, in_pairs, chain, counts, coords, tiles, keep_high, keep_low, send_high, send_low,
                 buf, coord_buf, spots, sems, acc):
    place_tiles(step, in_pairs, chain, counts, coords, tiles, buf, coord_buf, spots, sems, acc)

    @pl.loop(0, keep_high.shape[0] // ROWS_DEV)
    def _(chip):
        at = pl.multiple_of(chip * ROWS_DEV, ROWS_DEV)
        block_rows(acc, in_pairs, 2 * chip * BLOCKS_DEV, keep_high, keep_low, at)
        block_rows(acc, in_pairs, (2 * chip + 1) * BLOCKS_DEV, send_high, send_low, at)


def multiply(high, low, weights, start, out):
    span = pl.ds(start, out.shape[0])
    both = jnp.dot(high[span], weights[...], preferred_element_type=jnp.float32)
    rest = jnp.dot(low[span], weights[:, :QUERIES], preferred_element_type=jnp.float32)
    out[...] = both[:, :QUERIES] + (both[:, QUERIES:] + rest)


def leading_kernel(high, low, *refs):
    pieces, (out, weights) = refs[:-2], refs[-2:]
    for k, piece in enumerate(pieces):
        above, below = split(piece[...])
        weights[k * ROWS_DEV:(k + 1) * ROWS_DEV, :QUERIES] = above
        weights[k * ROWS_DEV:(k + 1) * ROWS_DEV, QUERIES:] = below
    multiply(high, low, weights, 0, out)


def product_kernel(start, high, low, weights, out):
    multiply(high, low, weights, start, out)


def shards(tiles, tile_coords, tile_count, seeds, chain):
    row_total = lax.axis_size("row")
    col_total = lax.axis_size("col")
    out_blocks = col_total * BLOCKS_DEV
    in_pairs = row_total
    depth_total = col_total // 2
    rows_out = depth_total * ROWS_DEV
    rows_in = in_pairs * LANES
    relations, pairs = tiles.shape[2], tiles.shape[3]
    f32, bf16 = jnp.float32, jnp.bfloat16

    tiles = tiles.reshape(relations, pairs, TILE, 2 * TILE)
    coords = tile_coords.reshape(relations, 2, 2 * pairs)
    seeds = seeds[None, :]

    smem = pl.BlockSpec(memory_space=pltpu.SMEM)
    vmem = pl.BlockSpec(memory_space=pltpu.VMEM)
    hbm = pl.BlockSpec(memory_space=pltpu.HBM)
    dense_bytes = out_blocks * in_pairs * TILE * LANES * 4
    tile_bytes = pairs * TILE * LANES * 4
    work = [
        pltpu.VMEM((pairs, TILE, 2 * TILE), f32),
        pltpu.VMEM((2, 2 * pairs), jnp.int32),
        pltpu.SMEM((1, 2 * pairs), jnp.int32),
        pltpu.SemaphoreType.DMA((MIN_SHARE + 1,)),
    ]
    sums = pltpu.VMEM((2 * out_blocks * in_pairs, TILE, LANES), f32)
    half = pltpu.VMEM((rows_out, rows_in), bf16)
    lead = pltpu.VMEM((ROWS_DEV, QUERIES), f32)
    rest = pltpu.VMEM((rows_out - ROWS_DEV, QUERIES), f32)
    last = pltpu.VMEM((rows_out - 2 * ROWS_DEV, QUERIES), f32)
    halved = pltpu.VMEM((rows_in, 2 * QUERIES), bf16)
    one_hot = pltpu.VMEM((rows_in, QUERIES), bf16)

    def limit(size):
        return pltpu.CompilerParams(vmem_limit_bytes=size + (2 << 20))

    def cost(flops):
        return pl.CostEstimate(flops=flops, bytes_accessed=1 << 20, transcendentals=0)

    def local(x):
        return pltpu.with_memory_space_constraint(x, pltpu.VMEM)

    def remain(x):
        return pltpu.with_memory_space_constraint(x, pltpu.HBM)

    given = [remain(x) for x in (chain, tile_count, seeds, coords, tiles)]

    def first():
        return pl.pallas_call(
            functools.partial(first_kernel, in_pairs, col_total),
            out_shape=[lead, sums, one_hot],
            in_specs=[smem, smem, vmem, hbm, hbm],
            out_specs=[vmem] * 3,
            scratch_shapes=work + [pltpu.VMEM((ROWS_DEV, rows_in), bf16)] * 2,
            compiler_params=limit(tile_bytes + dense_bytes // 2),
            name="first",
        )(*given)

    def one_hot_part(acc, states, away, turn, shape):
        return pl.pallas_call(
            functools.partial(one_hot_kernel, in_pairs, turn, away),
            out_shape=shape,
            in_specs=[vmem] * 2,
            out_specs=vmem,
            scratch_shapes=[pltpu.VMEM((shape.shape[0], rows_in), bf16)] * 2,
            compiler_params=limit(dense_bytes // 2),
            cost_estimate=cost(4 * shape.shape[0] * rows_in * QUERIES),
            name="one_hot_part",
        )(local(acc), local(states))

    def densify(step):
        return pl.pallas_call(
            functools.partial(dense_kernel, step, in_pairs),
            out_shape=[half] * 4,
            in_specs=[smem, smem, hbm, hbm],
            out_specs=[vmem] * 4,
            scratch_shapes=work + [sums],
            compiler_params=limit(tile_bytes + 2 * dense_bytes),
            cost_estimate=pl.CostEstimate(flops=0, bytes_accessed=8 << 20, transcendentals=0),
        )(*given[:2], *given[3:])

    def leading(high, low, pieces):
        return pl.pallas_call(
            leading_kernel,
            out_shape=[lead, halved],
            in_specs=[vmem] * (2 + len(pieces)),
            out_specs=[vmem] * 2,
            compiler_params=limit(4 << 20),
            cost_estimate=cost(6 * ROWS_DEV * rows_in * QUERIES),
            name="leading",
        )(local(high), local(low), *map(local, pieces))

    def product(high, low, weights, turn, shape):
        return pl.pallas_call(
            functools.partial(product_kernel, turn * ROWS_DEV),
            out_shape=shape,
            in_specs=[vmem] * 3,
            out_specs=vmem,
            compiler_params=limit(4 << 20),
            cost_estimate=cost(6 * shape.shape[0] * rows_in * QUERIES),
            name="product",
        )(local(high), local(low), local(weights))

    def swap(x, axis, size, flip):
        return lax.ppermute(x, axis, [(i, i ^ flip) for i in range(size)])

    def blocks_from(turn, away, shape):
        if step == 0:
            return one_hot_part(acc, states, away, turn, shape)
        return product(*relation[2 * away:2 * away + 2], weights, turn, shape)

    for step in range(HOPS):
        if step == 0:
            send, acc, states = first()
        else:
            send, weights = leading(*relation[2:], pieces)
        crossing = [swap(send, "col", col_total, 1)]
        send = blocks_from(1, 1, rest)
        crossing.append(swap(send, "col", col_total, 1))
        ready = [blocks_from(0, 0, lead) + crossing[0]]
        ready.append(blocks_from(1, 0, lead) + crossing[1][:ROWS_DEV])
        if depth_total > 2:
            tail = blocks_from(2, 0, last) + crossing[1][ROWS_DEV:]
            ready += [tail[k * ROWS_DEV:(k + 1) * ROWS_DEV] for k in range(depth_total - 2)]
        arrived = []
        for turn, flips in enumerate(zip(*visits(depth_total))):
            part = ready[turn]
            if turn == depth_total - 1:
                arrived.append(part)
                continue
            there = [(2 * z + core, 2 * (z ^ flips[core]) + core)
                     for z in range(depth_total) for core in range(2)]
            arrived.append(lax.ppermute(part, "col", there))
        if step + 1 < HOPS:
            following = densify(step + 1)
        owned = arrived[-1]
        for part in arrived[:-1]:
            owned = owned + part
        if step + 1 < HOPS:
            relation = following
            pieces = [owned] + [swap(owned, "row", row_total, k) for k in range(1, row_total)]

    squares = jnp.sum(owned * owned, axis=0, keepdims=True)
    devices = row_total * col_total
    shared = lax.all_to_all(
        jnp.broadcast_to(squares, (devices, QUERIES)), ("row", "col"), 0, 0, tiled=True)
    totals = jnp.sum(shared, axis=0)
    return owned * lax.rsqrt(totals / (devices * ROWS_DEV) + 1e-06)


def solution(mesh):
    in_specs = (
        P("row", "col", None, None, None, None),
        P("row", "col", None, None, None),
        P("row", "col", None),
        P(),
        P(),
    )
    out_specs = P(("row", "col"), None)
    return jax.shard_map(shards, mesh=mesh, in_specs=in_specs, out_specs=out_specs, check_vma=False)
```
